32 devices in a mesh: tensor: 4 (over x, core), seq: 4 (over z), dec: 2 (over y).
Axes of the slice: x: 2, y: 2, z: 4, core: 2. Of those that a mesh axis runs over, the one named last changes fastest.
Arguments:
- tokens: bfloat16 [2, 4, 1024, 2560], P('dec', 'seq', 'tensor'), may hold values from -320 to 320, as said below
- attn_gain: float32 [2560], replicated, may hold values from 0.1 to 1.9
- w_query: bfloat16 [2560, 2560], P(None, 'tensor'), may hold values from -2 to 8
- w_key: bfloat16 [2560, 640], replicated, may hold values from -2 to 8
- w_value: bfloat16 [2560, 640], replicated, may hold values from -4 to 4
- w_out: bfloat16 [2560, 2560], P('tensor'), may hold values from -0.125 to 0.125
- mlp_gain: float32 [2560], replicated, may hold values from 0.1 to 1.9
- w_gate: bfloat16 [2560, 6912], P(None, 'tensor'), may hold values from -0.125 to 0.125
- w_up: bfloat16 [2560, 6912], P(None, 'tensor'), may hold values from -0.125 to 0.125
- w_down: bfloat16 [6912, 2560], P('tensor'), may hold values from -0.078125 to 0.078125
- positions: int32 [2, 4, 1024], P('dec', 'seq'), may hold values from 0 to 4095, as said below
- window_lo: int32 [2, 4, 1024], P('dec', 'seq'), may hold values from 0 to 4095, as said below
- cache_pool: bfloat16 [320, 2, 16, 1280], P(('seq', 'dec'), None, 'tensor'), may hold values from -6 to 6
- req_len: int32 [8, 8], P(('seq', 'dec')), may hold values from 1 to 128, 512 in all within a row
- req_owner: int32 [64, 1], P(('seq', 'dec')), may hold values from 0 to 7, as said below
- block_list: int32 [8, 40], P(('seq', 'dec')), may hold values from 0 to 39, each once within a row
Outputs:
- layer_out: bfloat16 [2, 4, 1024, 2560], P('dec', 'seq', 'tensor')
- decode_cache: bfloat16 [128, 2, 16, 10240], P(('seq', 'dec'), None, 'tensor')
The draws below stay inside these ranges and needn't reach their ends.
Inputs may be any that keep to these rules, and one draw needn't show every extreme that they name: For the token at span index i: i - 4095 <= window_lo <= i; tokens of one document share their lower limit until the window binds. positions rise by one from token to token within a document. `req_len`: each source's 8 lengths sum to 512, and its longest is 128. `req_owner`: among the 8 requests of one source no owner is named more than 2 times, and one owner is named exactly 2 times by every source. Row-wise values of order one; some tokens may be far larger.
All inputs are finite; a program needn't handle non-finite values.
Results may differ from the reference program's by a relative error of at most 0.015.
Values may be sent and summed in bfloat16 or wider, within the bound.
No kernel may reach another device: no remote copies, remote signals or barrier semaphores. Data moves between devices by JAX's collectives and lax.ppermute only.
A program may use at most 384 MiB of HBM per device.

```python
import math
import jax
import jax.numpy as jnp
import numpy as np
from jax import lax

D = 2560
QH = 32
KVH = 8
HD = 80
FF = 6912
WINDOW = 4096
TOK_BLOCK = 1024
CACHE_LAYERS = 2
BT = 16
MAXLEN = 128
RQ = 8
PAIR = 2
SEQS = 2
SEQ_BLOCKS = 4
SPAN = 4096
KVP = 16
OWNERS = 8
TOTAL = 512
NB = 40
POOL = 320
SLOTS = 128
N_TENSOR = 4


def draw_tokens(key, part):
    shape_all = (SEQS, SEQ_BLOCKS, TOK_BLOCK, D)
    key_base = jax.random.fold_in(key, 0)
    values = jax.random.normal(key_base, shape_all, jnp.float32)
    return values.astype(jnp.bfloat16)


def spiked_weight(key, columns):
    scale_in = D ** (-0.5)
    values = jnp.clip(jax.random.normal(key, (D, columns), jnp.float32), -6.0, 6.0) * scale_in
    return values.astype(jnp.bfloat16)


def draw_w_query(key, part):
    return spiked_weight(jax.random.fold_in(key, 31), QH * HD)


def draw_w_key(key, part):
    return spiked_weight(jax.random.fold_in(key, 37), KVH * HD)


def document_layout(key):
    base_key = jax.random.fold_in(key, 4711)
    key_cut = jax.random.fold_in(base_key, 0)
    index_all = jnp.broadcast_to(jnp.arange(SPAN, dtype=jnp.int32)[None, :], (SEQS, SPAN))
    cuts = jax.random.randint(key_cut, (SEQS, SPAN), 0, max(2, TOK_BLOCK // 2)) == 0
    cuts = cuts & (index_all >= 2 * TOK_BLOCK) | (index_all == 0) | (index_all == SPAN - 1)
    doc_start = lax.cummax(jnp.where(cuts, index_all, 0), axis=1)
    first_len = jnp.sum((doc_start == 0).astype(jnp.int32), axis=1, keepdims=True)
    offset = (SPAN - first_len).astype(jnp.int32)
    places = index_all - doc_start + jnp.where(doc_start == 0, offset, 0)
    lower = jnp.maximum(doc_start, index_all - WINDOW + 1)
    return (places.reshape(SEQS, SEQ_BLOCKS, TOK_BLOCK).astype(jnp.int32), lower.reshape(SEQS, SEQ_BLOCKS, TOK_BLOCK).astype(jnp.int32))


def draw_positions(key, part):
    return document_layout(key)[0]


def draw_window_lo(key, part):
    return document_layout(key)[1]


def draw_req_owner(key, part):
    hot_key, rest_key = jax.random.split(jax.random.fold_in(key, 17))
    hot_owner = jax.random.randint(hot_key, (), 0, OWNERS)

    def per_source(source_key):
        key_pick, key_order = jax.random.split(source_key)
        slot_ids = jax.random.permutation(key_pick, (OWNERS - 1) * PAIR)[:RQ - PAIR]
        others = slot_ids // PAIR
        others = others + (others >= hot_owner).astype(others.dtype)
        listed = jnp.concatenate([jnp.full((PAIR,), hot_owner, others.dtype), others])
        return listed[jax.random.permutation(key_order, RQ)]
    source_keys = jax.random.split(rest_key, OWNERS)
    return jax.vmap(per_source)(source_keys).reshape(OWNERS * RQ, 1).astype(jnp.int32)


def steps_of(own_key, shape, shards, least, high):
    def one(position, blocks):
        heights = jax.random.uniform(jax.random.fold_in(jax.random.fold_in(own_key, 6), position), (blocks,), jnp.float32, least / len(shards), high / len(shards))
        return jnp.repeat(jnp.exp(heights), shape[position] // blocks).reshape((-1,) + (1,) * (len(shape) - position - 1))

    loudness = one(*shards[0])
    for cut in shards[1:]:
        loudness = loudness * one(*cut)
    return loudness


def profile(amount, total, bound, lean):
    weights = [(1 << 20) // math.isqrt(grade ** lean) + 1 for grade in range(2, amount + 1)]
    rest, given = total - bound - (amount - 1), [1] * (amount - 1)
    while rest > 0:
        candidates = [i for i in range(amount - 1) if given[i] < bound]
        mass, left = sum([weights[i] for i in candidates]), rest
        for i in candidates:
            extra = min(bound - given[i], max(1, left * weights[i] // mass), rest)
            given[i] = given[i] + extra
            rest = rest - extra
    return np.array([bound] + given)


def uneven_parts(rng, count, total, reach, slope):
    if count == 2:
        one = jax.random.randint(rng, (), max(1, total - reach), min(reach, total - 1) + 1)
        return jnp.stack([one, total - one])
    sizes = jnp.asarray(profile(count, total, reach, slope), jnp.int32)
    pairs = (count - 1) // 2
    source_of, sink = sizes[1:1 + 2 * pairs:2], sizes[2:2 + 2 * pairs:2]
    room = jnp.minimum(source_of - 1, reach - sink)
    shifted = jax.random.randint(jax.random.fold_in(rng, 1), (pairs,), 0, 1 << 20) % (room + 1)
    sizes = sizes.at[1:1 + 2 * pairs:2].set(source_of - shifted).at[2:2 + 2 * pairs:2].set(sink + shifted)
    return sizes[jax.random.permutation(jax.random.fold_in(rng, 2), count)]


def scatter_about(own_key, shape, deviation, bound, cuts=(), kind=jnp.bfloat16):
    drawn = deviation * jax.random.normal(own_key, shape, jnp.float32)
    if cuts:
        drawn = drawn * steps_of(own_key, shape, cuts, -0.22, 0.18)
    return jnp.clip(drawn, -bound, bound).astype(kind)


def setup_inputs(seed: int = 0) -> dict:
    seeds = jax.random.split(jax.random.key(seed), 17)
    return {
        "tokens": draw_tokens(jax.random.fold_in(seeds[16], 71), 0),
        "attn_gain": jnp.clip(1.0 + 0.18 * jax.random.normal(seeds[1], (D,), jnp.float32), 0.1, 1.9),
        "w_query": draw_w_query(jax.random.fold_in(seeds[16], 71), 0),
        "w_key": draw_w_key(jax.random.fold_in(seeds[16], 71), 0),
        "w_value": scatter_about(seeds[4], (D, KVH * HD), 0.3, 4.0),
        "w_out": scatter_about(seeds[5], (QH * HD, D), (QH * HD) ** -0.5, 0.125, ((0, 4),)),
        "mlp_gain": jnp.clip(1.0 + 0.18 * jax.random.normal(seeds[6], (D,), jnp.float32), 0.1, 1.9),
        "w_gate": scatter_about(seeds[7], (D, FF), D ** -0.5, 0.125, ((1, 4),)),
        "w_up": scatter_about(seeds[8], (D, FF), D ** -0.5, 0.125, ((1, 4),)),
        "w_down": scatter_about(seeds[9], (FF, D), FF ** -0.5, 0.078125, ((0, 4),)),
        "positions": draw_positions(jax.random.fold_in(seeds[16], 71), 0),
        "window_lo": draw_window_lo(jax.random.fold_in(seeds[16], 71), 0),
        "cache_pool": scatter_about(seeds[12], (POOL, CACHE_LAYERS, KVP, BT * HD), 1.0, 6.0, ((0, 8), (2, 4))),
        "req_len": jax.vmap(lambda own: uneven_parts(own, RQ, TOTAL, MAXLEN, 2))(jax.random.split(seeds[13], OWNERS)).reshape((OWNERS, RQ)).astype(jnp.int32),
        "req_owner": draw_req_owner(jax.random.fold_in(seeds[16], 71), 0),
        "block_list": jax.vmap(lambda own: jax.random.permutation(own, NB))(jax.random.split(seeds[15], OWNERS)).reshape((OWNERS, NB)).astype(jnp.int32),
    }


norm_eps = 1e-05
rope_base = 10000.0

def rms_scale(row_block, gain_vec):
    values = row_block.astype(jnp.float32)
    mean_square = lax.optimization_barrier(jnp.mean(values * values, axis=-1, keepdims=True))
    return values * lax.rsqrt(mean_square + norm_eps) * gain_vec.astype(jnp.float32)

def rotate(values, places):
    half_dim = values.shape[-1] // 2
    inverse_rate = jnp.power(jnp.float32(rope_base), -(2.0 * jnp.arange(half_dim, dtype=jnp.float32)) / values.shape[-1])
    angles = places.astype(jnp.float32)[:, None] * inverse_rate[None, :]
    cosine = jnp.cos(angles)[:, None, :]
    sine_vals = jnp.sin(angles)[:, None, :]
    first_half = values[..., :half_dim]
    second = values[..., half_dim:]
    return jnp.concatenate([first_half * cosine - second * sine_vals, second * cosine + first_half * sine_vals], axis=-1)

def shard_sum(left, right, width):
    accum = jnp.zeros((left.shape[0], right.shape[1]), jnp.float32)
    for shard_num in range(left.shape[1] // width):
        part_sum = jnp.dot(left[:, shard_num * width:(shard_num + 1) * width], right[shard_num * width:(shard_num + 1) * width], preferred_element_type=jnp.float32)
        rounded = lax.optimization_barrier(part_sum.astype(jnp.bfloat16))
        accum = accum + rounded.astype(jnp.float32)
    return accum

def attend(queries, keys_rot, values_in, lower):
    qblock = min(512, TOK_BLOCK)
    group_size = QH // KVH
    padded_keys = jnp.concatenate([jnp.zeros((WINDOW, KVH, HD), jnp.bfloat16), keys_rot], axis=0)
    padded_values = jnp.concatenate([jnp.zeros((WINDOW, KVH, HD), jnp.bfloat16), values_in], axis=0)

    def one_block(block_begin):
        q_part = lax.dynamic_slice_in_dim(queries, block_begin, qblock, 0).reshape(qblock, KVH, group_size, HD)
        k_part = lax.dynamic_slice_in_dim(padded_keys, block_begin, WINDOW + qblock, 0)
        v_part = lax.dynamic_slice_in_dim(padded_values, block_begin, WINDOW + qblock, 0)
        scores = jnp.einsum('qcgd,kcd->cgqk', q_part.astype(jnp.float32), k_part.astype(jnp.float32)) * HD ** (-0.5)
        query_pos = block_begin + jnp.arange(qblock, dtype=jnp.int32)
        key_pos = block_begin - WINDOW + jnp.arange(WINDOW + qblock, dtype=jnp.int32)
        low_bound = lax.dynamic_slice_in_dim(lower, block_begin, qblock, 0)
        visible = (key_pos[None, :] >= low_bound[:, None]) & (key_pos[None, :] <= query_pos[:, None])
        scores = jnp.where(visible[None, None], scores, -jnp.inf)
        row_top = lax.optimization_barrier(jnp.max(scores, axis=-1, keepdims=True))
        exp_scores = jnp.exp(scores - row_top)
        row_total = lax.optimization_barrier(jnp.sum(exp_scores, axis=-1, keepdims=True))
        weights = (exp_scores / row_total).astype(jnp.bfloat16)
        mixed_vals = jnp.einsum('cgqk,kcd->qcgd', weights.astype(jnp.float32), v_part.astype(jnp.float32))
        return mixed_vals.reshape(qblock, QH * HD).astype(jnp.bfloat16)
    block_starts = jnp.arange(SPAN // qblock, dtype=jnp.int32) * qblock
    return lax.map(one_block, block_starts).reshape(SPAN, QH * HD)

def layer_span(row_block, attn_gain, w_query, w_key, w_value, w_out, mlp_gain, w_gate, w_up, w_down, places, lower):
    normed_in = rms_scale(row_block, attn_gain).astype(jnp.bfloat16)
    queries = rotate(jnp.dot(normed_in, w_query, preferred_element_type=jnp.float32).reshape(SPAN, QH, HD), places).astype(jnp.bfloat16)
    keys_rot = rotate(jnp.dot(normed_in, w_key, preferred_element_type=jnp.float32).reshape(SPAN, KVH, HD), places).astype(jnp.bfloat16)
    values_in = jnp.dot(normed_in, w_value, preferred_element_type=jnp.float32).reshape(SPAN, KVH, HD).astype(jnp.bfloat16)
    heads = attend(queries, keys_rot, values_in, lower)
    attn = shard_sum(heads, w_out, QH * HD // N_TENSOR)
    residual = row_block.astype(jnp.float32) + attn
    mixed_in = rms_scale(residual, mlp_gain).astype(jnp.bfloat16)
    gate_vals = jnp.dot(mixed_in, w_gate, preferred_element_type=jnp.float32)
    up_vals = jnp.dot(mixed_in, w_up, preferred_element_type=jnp.float32)
    hidden = (jax.nn.silu(gate_vals) * up_vals).astype(jnp.bfloat16)
    return (residual + shard_sum(hidden, w_down, FF // N_TENSOR)).astype(jnp.bfloat16)

def hand_over(cache_pool, req_len, req_owner, block_list):
    max_blocks = MAXLEN // BT
    result = jnp.zeros((SLOTS, CACHE_LAYERS, KVP, MAXLEN * HD), jnp.bfloat16)
    req_order = jnp.arange(RQ, dtype=jnp.int32)
    token_idx = jnp.arange(max_blocks, dtype=jnp.int32)[:, None] * BT + jnp.arange(BT, dtype=jnp.int32)[None, :]
    for source in range(OWNERS):
        lengths = req_len[source].astype(jnp.int32)
        owner_ids = req_owner[source * RQ:(source + 1) * RQ, 0].astype(jnp.int32)
        listing = block_list[source].astype(jnp.int32)
        counts = (lengths + BT - 1) // BT
        first_block = (jnp.cumsum(counts) - counts).astype(jnp.int32)
        same_owner = (owner_ids[:, None] == owner_ids[None, :]) & (req_order[None, :] < req_order[:, None])
        arrival = lax.optimization_barrier(jnp.sum(same_owner.astype(jnp.int32), axis=1)).astype(jnp.int32)
        block_idx = jnp.minimum(first_block[:, None] + jnp.arange(max_blocks, dtype=jnp.int32)[None, :], NB - 1)
        pool_rows = (source * NB + listing[block_idx]).astype(jnp.int32)
        picked = cache_pool[pool_rows].reshape(RQ, max_blocks, CACHE_LAYERS, KVP, BT, HD)
        keep_mask = token_idx[None] < lengths[:, None, None]
        picked = jnp.where(keep_mask[:, :, None, None, :, None], picked, jnp.zeros((), jnp.bfloat16))
        arranged = jnp.transpose(picked, (0, 2, 3, 1, 4, 5)).reshape(RQ, CACHE_LAYERS, KVP, MAXLEN * HD)
        dest_rows = (owner_ids * (OWNERS * PAIR) + source * PAIR + arrival).astype(jnp.int32)
        result = result.at[dest_rows].set(arranged)
    return result

def reference(tokens, attn_gain, w_query, w_key, w_value, w_out, mlp_gain, w_gate, w_up, w_down, positions, window_lo, cache_pool, req_len, req_owner, block_list):
    outputs = []
    for seq_num in range(SEQS):
        outputs.append(layer_span(tokens[seq_num].reshape(SPAN, D), attn_gain, w_query, w_key, w_value, w_out, mlp_gain, w_gate, w_up, w_down, positions[seq_num].reshape(SPAN), window_lo[seq_num].reshape(SPAN)))
    layer_out = jnp.stack(outputs).reshape(SEQS, SEQ_BLOCKS, TOK_BLOCK, D)
    return (layer_out, hand_over(cache_pool, req_len, req_owner, block_list))
```

```python
import functools
import math

import jax
import jax.numpy as jnp
import numpy as np
from jax import lax
from jax.experimental import pallas as pl
from jax.experimental.pallas import tpu as pltpu
from jax.sharding import PartitionSpec as P


QH = 32
KVH = 8
HD = 80
WINDOW = 4096
BT = 16
MAXLEN = 128
PAIR = 2
QT = 128
NEG = -0.7 * float(np.finfo(np.float32).max)
EXP_SCALE = HD ** (-0.5) * math.log2(math.e)

norm_eps = 1e-05
rope_base = 10000.0

MIB = 1024 * 1024


def flip(value, axis, bit):
    axes = axis if isinstance(axis, tuple) else (axis,)
    count = math.prod(lax.axis_size(a) for a in axes)
    return lax.ppermute(value, axis, [(i, i ^ bit) for i in range(count)])


def rms_scale(values, gain_vec):
    mean_square = jnp.mean(values * values, axis=-1, keepdims=True)
    return values * lax.rsqrt(mean_square + norm_eps) * gain_vec


def qkv_kernel(place_ref, *refs, parts, heads, kv_count, pieces, offsets, block_rows):
    x_refs = refs[:parts]
    gain_ref, wq_ref, wk0_ref, wk1_ref, wv0_ref, wv1_ref, cos_ref, sin_ref = refs[parts : parts + 8]
    q_ref, kv_ref, k_s, v_s = refs[parts + 8 :]
    half = HD // 2
    t_index = place_ref[0]
    shift = place_ref[3]
    wk = jnp.concatenate([wk0_ref[...], wk1_ref[...]], axis=1)
    wv = jnp.concatenate([wv0_ref[...], wv1_ref[...]], axis=1)
    lane = 0
    for p in range(parts):
        rows = x_refs[p].shape[0]
        normed = rms_scale(x_refs[p][...].astype(jnp.float32), gain_ref[...]).astype(jnp.bfloat16)
        at = jnp.bitwise_xor(t_index, pieces[p]) * block_rows + offsets[p]
        at = pl.multiple_of(at, QT)
        cosine = cos_ref[:, pl.ds(at, rows)]
        sine = sin_ref[:, pl.ds(at, rows)]
        here = slice(lane, lane + rows)

        def turned(first, second):
            return jnp.concatenate(
                [
                    (first * cosine - second * sine).astype(jnp.bfloat16),
                    (second * cosine + first * sine).astype(jnp.bfloat16),
                ],
                axis=0,
            )

        k_s[:, :rows] = jnp.dot(normed, wk, preferred_element_type=jnp.float32).T
        v_s[:, :rows] = jnp.dot(normed, wv, preferred_element_type=jnp.float32).T
        for h in range(kv_count):
            row = pl.multiple_of(shift + h * HD, 8)
            kv_ref[h * HD : (h + 1) * HD, here] = turned(
                k_s[pl.ds(row, half), :rows], k_s[pl.ds(pl.multiple_of(row + half, 8), half), :rows]
            )
            kv_ref[(kv_count + h) * HD : (kv_count + h + 1) * HD, here] = v_s[
                pl.ds(row, HD), :rows
            ].astype(jnp.bfloat16)
        q_t = jnp.dot(normed, wq_ref[...], preferred_element_type=jnp.float32).T
        for h in range(heads):
            row = h * HD
            q_ref[row : row + HD, here] = turned(q_t[row : row + half], q_t[row + half : row + HD])
        lane += rows


def project(place, xs, pieces, offsets, block_rows, gain, w_q, w_k, w_v, cos_t, sin_t, heads, kv_count):
    width = xs[0].shape[1]
    rows = sum(x.shape[0] for x in xs)
    most = max(x.shape[0] for x in xs)
    qw, kvw = heads * HD, 2 * kv_count * HD
    whole = lambda i, place_ref: (0, 0)
    lead = pl.BlockSpec((width, 128), lambda i, place_ref: (0, place_ref[2]))
    after = pl.BlockSpec((width, 128), lambda i, place_ref: (0, place_ref[2] + 1))
    return pl.pallas_call(
        functools.partial(
            qkv_kernel,
            parts=len(xs),
            heads=heads,
            kv_count=kv_count,
            pieces=pieces,
            offsets=offsets,
            block_rows=block_rows,
        ),
        grid_spec=pltpu.PrefetchScalarGridSpec(
            num_scalar_prefetch=1,
            grid=(1,),
            in_specs=[pl.BlockSpec(x.shape, whole) for x in xs]
            + [pl.BlockSpec((1, width), whole), pl.BlockSpec((width, qw), whole)]
            + [lead, after, lead, after]
            + [pl.BlockSpec(cos_t.shape, whole)] * 2,
            out_specs=[pl.BlockSpec((qw, rows), whole), pl.BlockSpec((kvw, rows), whole)],
            scratch_shapes=[pltpu.VMEM((256, most), jnp.float32)] * 2,
        ),
        out_shape=[
            jax.ShapeDtypeStruct((qw, rows), jnp.bfloat16),
            jax.ShapeDtypeStruct((kvw, rows), jnp.bfloat16),
        ],
        compiler_params=pltpu.CompilerParams(vmem_limit_bytes=36 * MIB),
        name="qkv",
    )(place, *xs, gain, w_q, w_k, w_k, w_v, w_v, cos_t, sin_t)


def attn_kernel(
    place_ref, min_ref, max_ref, *refs, groups, per, n, rows, block_len, order, chunk, chunks, layout
):
    distances = len(layout)
    count = sum(len(group) for group in layout)
    q1_ref, q2_ref, low_ref = refs[:3]
    kv_hbm = refs[3 : 3 + count]
    out_ref = refs[3 + count]
    kv_s, q_s, m_s, acc_s, sem = refs[4 + count :]
    i = pl.program_id(0)
    t_index = place_ref[0]
    seq_index = place_ref[1]

    def copies():
        found = []
        ref = 0
        for d in range(distances):
            for spans in layout[d]:
                for src, dst, size in spans:
                    found.append(
                        pltpu.make_async_copy(
                            kv_hbm[ref].at[:, pl.ds(src, size)],
                            kv_s.at[d, :, pl.ds(dst, size)],
                            sem.at[len(found)],
                        )
                    )
                ref += 1
        return found

    @pl.when(i == 0)
    def _():
        for copy in copies():
            copy.start()

    piece = jnp.int32(order[0])
    for k in range(1, n):
        piece = jnp.where(i == k, order[k], piece)

    def fetch(q_ref):
        for g in range(groups):
            for h in range(per):
                r = (g * per + h) * HD
                q_s[g, :, h * QT : (h + 1) * QT] = q_ref[r : r + HD, :]

    @pl.when(piece < n // 2)
    def _():
        fetch(q1_ref)

    @pl.when(piece >= n // 2)
    def _():
        fetch(q2_ref)

    m_s[...] = jnp.full_like(m_s, NEG)
    acc_s[...] = jnp.zeros_like(acc_s)

    @pl.when(i == 0)
    def _():
        for copy in copies():
            copy.wait()

    place_of = jnp.bitwise_xor(t_index, piece)
    q_first = seq_index * block_len + place_of * rows + chunk * QT
    low_min = min_ref[place_of * chunks + chunk]
    low_max = max_ref[place_of * chunks + chunk]
    low_at = pl.multiple_of(place_of * rows + chunk * QT, QT)
    ones = jnp.ones((16, rows), jnp.bfloat16)

    def tile_step(d, lane, base, masked):
        if masked:
            key_pos = base + lax.broadcasted_iota(jnp.int32, (rows, QT), 0)
            query_pos = q_first + lax.broadcasted_iota(jnp.int32, (rows, QT), 1)
            seen = (key_pos >= low_ref[:, pl.ds(low_at, QT)]) & (key_pos <= query_pos)
            bias = jnp.where(seen, 0.0, NEG)
            bias = jnp.concatenate([bias] * per, axis=1)
        olds = [m_s[g] for g in range(groups)]
        scores = []
        for g in range(groups):
            k_t = kv_s[d, g * HD : (g + 1) * HD, pl.ds(lane, rows)]
            part = lax.dot_general(
                k_t, q_s[g], (((0,), (0,)), ((), ())), preferred_element_type=jnp.float32
            )
            scores.append(part + bias if masked else part)
        for g in range(groups):
            v_t = kv_s[d, (groups + g) * HD : (groups + g + 1) * HD, pl.ds(lane, rows)]
            m_new = jnp.maximum(olds[g], jnp.max(scores[g], axis=0, keepdims=True))
            probs = jnp.exp2((scores[g] - m_new) * EXP_SCALE).astype(jnp.bfloat16)
            scale = jnp.exp2((olds[g] - m_new) * EXP_SCALE)
            mixed = jnp.dot(
                jnp.concatenate([v_t, ones], axis=0), probs, preferred_element_type=jnp.float32
            )
            m_s[g] = m_new
            acc_s[g] = acc_s[g] * scale + mixed

    first_tile = lax.div(low_min, rows)
    last_tile = lax.div(q_first + QT - 1, rows)

    def step(tile, carry):
        block = lax.div(tile, n)
        d = seq_index - block
        lane = pl.multiple_of(jnp.bitwise_xor(t_index, tile - block * n) * rows, rows)
        base = tile * rows
        whole = (base + rows - 1 <= q_first) & (base >= low_max)

        @pl.when(whole)
        def _():
            tile_step(d, lane, base, False)

        @pl.when(jnp.logical_not(whole))
        def _():
            tile_step(d, lane, base, True)

        return carry

    lax.fori_loop(first_tile, last_tile + 1, step, 0)
    parts = []
    for g in range(groups):
        acc = acc_s[g]
        share = acc[:HD] / acc[HD : HD + 1]
        for h in range(per):
            parts.append(share[:, h * QT : (h + 1) * QT])
    out_ref[...] = jnp.concatenate(parts, axis=0).T.astype(jnp.bfloat16)


def attend(place, low_min, low_max, q1, q2, lower, kv_lists, layout, groups, per, n, rows, order, chunk, chunks):
    width = groups * per * HD
    block_len = lower.shape[1]
    m = n // 2
    kv_flat = [kv for held in kv_lists for kv in held]
    copies = sum(len(spans) for group in layout for spans in group)

    def table(values):
        def at(i, *_):
            found = jnp.int32(values[0])
            for k in range(1, n):
                found = jnp.where(i == k, values[k], found)
            return (0, found)

        return at

    first_lane = [(j % m) * chunks + chunk for j in order]
    second_lane = [j % m for j in order]
    return pl.pallas_call(
        functools.partial(
            attn_kernel,
            groups=groups,
            per=per,
            n=n,
            rows=rows,
            block_len=block_len,
            order=order,
            chunk=chunk,
            chunks=chunks,
            layout=layout,
        ),
        grid_spec=pltpu.PrefetchScalarGridSpec(
            num_scalar_prefetch=3,
            grid=(n,),
            in_specs=[
                pl.BlockSpec((width, QT), table(first_lane)),
                pl.BlockSpec((width, QT), table(second_lane)),
                pl.BlockSpec((1, block_len), lambda i, *_: (0, 0)),
            ]
            + [pl.BlockSpec(memory_space=pl.ANY)] * len(kv_flat),
            out_specs=pl.BlockSpec((QT, width), lambda i, *_: (i, 0)),
            scratch_shapes=[
                pltpu.VMEM((len(kv_lists), 2 * groups * HD, block_len), jnp.bfloat16),
                pltpu.VMEM((groups, HD, per * QT), jnp.bfloat16),
                pltpu.VMEM((groups, 1, per * QT), jnp.float32),
                pltpu.VMEM((groups, HD + 16, per * QT), jnp.float32),
                pltpu.SemaphoreType.DMA((copies,)),
            ],
        ),
        out_shape=jax.ShapeDtypeStruct((n * QT, width), jnp.bfloat16),
        compiler_params=pltpu.CompilerParams(vmem_limit_bytes=20 * MIB),
        name="attend",
    )(place, low_min, low_max, q1, q2, lower, *kv_flat)


def merge_kernel(own_ref, crossed_ref, mine_ref, theirs_ref, gain_ref, residual_ref, mixed_ref):
    first = mine_ref[:QT].astype(jnp.float32) + theirs_ref[QT:].astype(jnp.float32)
    residual = own_ref[...].astype(jnp.float32) + first
    residual_ref[...] = residual
    mixed_ref[:QT] = rms_scale(residual, gain_ref[...]).astype(jnp.bfloat16)
    second = mine_ref[QT:].astype(jnp.float32) + theirs_ref[:QT].astype(jnp.float32)
    residual = crossed_ref[...].astype(jnp.float32) + second
    mixed_ref[QT:] = rms_scale(residual, gain_ref[...]).astype(jnp.bfloat16)


def merge(own, chunk, crossed, mine, theirs, gain):
    width = own.shape[1]
    whole = lambda i: (0, 0)
    return pl.pallas_call(
        merge_kernel,
        grid=(1,),
        in_specs=[
            pl.BlockSpec((QT, width), lambda i: (chunk, 0)),
            pl.BlockSpec((QT, width), whole),
            pl.BlockSpec((2 * QT, width), whole),
            pl.BlockSpec((2 * QT, width), whole),
            pl.BlockSpec((1, width), whole),
        ],
        out_specs=[pl.BlockSpec((QT, width), whole), pl.BlockSpec((2 * QT, width), whole)],
        out_shape=[
            jax.ShapeDtypeStruct((QT, width), jnp.float32),
            jax.ShapeDtypeStruct((2 * QT, width), jnp.bfloat16),
        ],
        compiler_params=pltpu.CompilerParams(vmem_limit_bytes=20 * MIB),
        name="merge",
    )(own, crossed, mine, theirs, gain)


def unit_spans(units):
    spans = []
    at = 0
    size = 256
    while at < units:
        size = min(size, units - at)
        spans.append((at, size))
        at += size
        size = 512
    return spans


def ffn_kernel(*refs, parts):
    x_hbm = refs[:parts]
    gate_hbm, up_hbm, down_hbm, sent_ref, kept_ref = refs[parts : parts + 5]
    x_s, wg_s, wu_s, wd_s, sum_s, sem = refs[parts + 5 :]
    part_rows = x_hbm[0].shape[0]
    spans = unit_spans(wd_s.shape[0])

    def rows_copy(src, dst, span, index):
        here = pl.ds(*span)
        return pltpu.make_async_copy(src.at[here], dst.at[here], sem.at[index])

    x_copies = [
        pltpu.make_async_copy(x_hbm[p], x_s.at[pl.ds(p * part_rows, part_rows)], sem.at[p])
        for p in range(parts)
    ]
    weight_copies = [
        [
            rows_copy(src, dst, span, parts + 3 * k + w)
            for w, (src, dst) in enumerate(((gate_hbm, wg_s), (up_hbm, wu_s), (down_hbm, wd_s)))
        ]
        for k, span in enumerate(spans)
    ]
    for copy in x_copies:
        copy.start()
    for copies in weight_copies:
        for copy in copies:
            copy.start()
    for copy in x_copies:
        copy.wait()
    x = x_s[...]
    turned = (((1,), (1,)), ((), ()))
    half = sent_ref.shape[0]
    for k, (at, size) in enumerate(spans):
        for copy in weight_copies[k]:
            copy.wait()
        here = slice(at, at + size)
        gate = lax.dot_general(x, wg_s[here], turned, preferred_element_type=jnp.float32)
        up = lax.dot_general(x, wu_s[here], turned, preferred_element_type=jnp.float32)
        hidden = (gate * (1.0 / (1.0 + jnp.exp(-gate))) * up).astype(jnp.bfloat16)
        part = jnp.dot(hidden, wd_s[here], preferred_element_type=jnp.float32)
        if k == 0:
            sum_s[...] = part
        elif k < len(spans) - 1:
            sum_s[...] += part
        else:
            sent_ref[...] = (sum_s[:half] + part[:half]).astype(jnp.bfloat16)
            kept_ref[...] = (sum_s[half:] + part[half:]).astype(jnp.bfloat16)


def feed_forward(xs, w_gate, w_up, w_down):
    width, units = w_gate.shape
    rows = sum(x.shape[0] for x in xs)
    any_spec = pl.BlockSpec(memory_space=pl.ANY)
    vmem_spec = pl.BlockSpec(memory_space=pltpu.VMEM)
    return pl.pallas_call(
        functools.partial(ffn_kernel, parts=len(xs)),
        in_specs=[any_spec] * (len(xs) + 3),
        out_specs=[vmem_spec, vmem_spec],
        out_shape=[jax.ShapeDtypeStruct((rows // 2, width), jnp.bfloat16)] * 2,
        scratch_shapes=[
            pltpu.VMEM((rows, width), jnp.bfloat16),
            pltpu.VMEM((units, width), jnp.bfloat16),
            pltpu.VMEM((units, width), jnp.bfloat16),
            pltpu.VMEM((units, width), jnp.bfloat16),
            pltpu.VMEM((rows, width), jnp.float32),
            pltpu.SemaphoreType.DMA((len(xs) + 3 * len(unit_spans(units)),)),
        ],
        compiler_params=pltpu.CompilerParams(vmem_limit_bytes=56 * MIB),
        name="ffn",
    )(*xs, w_gate.T, w_up.T, w_down)


def pack_kernel(me_ref, len_ref, own_ref, list_ref, pool_ref, out_ref, *, req_count, pool_len):
    owner = jnp.bitwise_xor(me_ref[0], pl.program_id(0))
    feats = pool_ref.shape[-1]
    token_width = feats // BT
    lens = [jnp.int32(0)] * PAIR
    firsts = [jnp.int32(0)] * PAIR
    seen = jnp.int32(0)
    block = jnp.int32(0)
    for k in range(req_count):
        mine = own_ref[k, 0] == owner
        for r in range(PAIR):
            take = mine & (seen == r)
            lens[r] = jnp.where(take, len_ref[0, k], lens[r])
            firsts[r] = jnp.where(take, block, firsts[r])
        seen = seen + mine.astype(jnp.int32)
        block = block + lax.div(len_ref[0, k] + BT - 1, BT)
    for r in range(PAIR):
        for b in range(MAXLEN // BT):
            left = lens[r] - b * BT
            row = list_ref[0, jnp.minimum(firsts[r] + b, pool_len - 1)]
            where = (0, r, slice(None), slice(None), slice(b * feats, (b + 1) * feats))

            @pl.when(left >= BT)
            def _():
                out_ref[where] = pool_ref[row]

            @pl.when(left <= 0)
            def _():
                out_ref[where] = jnp.zeros(pool_ref.shape[1:], jnp.bfloat16)

            @pl.when((left > 0) & (left < BT))
            def _():
                data = pool_ref[row].astype(jnp.float32)
                lanes = lax.broadcasted_iota(jnp.int32, data.shape, 2)
                out_ref[where] = jnp.where(lanes < left * token_width, data, 0.0).astype(jnp.bfloat16)


def pack_cache(me, cache_pool, req_len, req_owner, block_list, owners):
    pool_len, layers, pieces, feats = cache_pool.shape
    req_count = req_len.shape[1]
    width = feats * (MAXLEN // BT)
    smem = pl.BlockSpec(memory_space=pltpu.SMEM)
    return pl.pallas_call(
        functools.partial(pack_kernel, req_count=req_count, pool_len=pool_len),
        grid=(owners,),
        in_specs=[smem, smem, smem, smem, pl.BlockSpec(cache_pool.shape, lambda k: (0, 0, 0, 0))],
        out_specs=pl.BlockSpec((1, PAIR, layers, pieces, width), lambda k: (k, 0, 0, 0, 0)),
        out_shape=jax.ShapeDtypeStruct((owners, PAIR, layers, pieces, width), jnp.bfloat16),
        compiler_params=pltpu.CompilerParams(vmem_limit_bytes=16 * MIB),
        name="pack",
    )(me, req_len, req_owner, block_list, cache_pool)


def piece_order(n):
    order = [0, n // 2]
    bit = n // 4
    while bit >= 1:
        order = [j | bit for j in order] + order
        bit //= 2
    return order


def low_bits(n):
    bits = []
    bit = 1
    while bit < n // 2:
        bits.append(bit)
        bit *= 2
    return bits


def gather_low(value, n):
    held = {0: value}
    for bit in reversed(low_bits(n)):
        for j in sorted(held):
            held[j | bit] = flip(held[j], "tensor", bit)
    return [held[j] for j in range(n // 2)]


def reduce_low(sent, kept, n):
    bits = low_bits(n)
    value = kept.astype(jnp.float32) + flip(sent, "tensor", bits[0]).astype(jnp.float32)
    for bit in bits[1:]:
        half = value.shape[0] // 2
        got = flip(value[:half].astype(jnp.bfloat16), "tensor", bit)
        value = value[half:] + got.astype(jnp.float32)
    return value


def layer(own, attn_gain, w_query, w_key, w_value, w_out, mlp_gain, w_gate, w_up, w_down, places, lower):
    n = lax.axis_size("tensor")
    seq_count = lax.axis_size("seq")
    rows, width = own.shape
    block_len = places.shape[0]
    t_index = lax.axis_index("tensor")
    seq_index = lax.axis_index("seq")
    heads = w_query.shape[1] // HD
    per = min(heads, QH // KVH)
    groups = heads // per
    m = n // 2
    chunks = rows // QT
    order = piece_order(n)
    reach = min(WINDOW // block_len, seq_count - 1)
    gain_in = attn_gain.reshape(1, width)
    gain_mlp = mlp_gain.reshape(1, width)

    crossed = []
    for c in range(chunks):
        crossed.append(flip(own[c * QT : (c + 1) * QT], "tensor", m))
    first_half = gather_low(own, n)

    kv_col = (t_index * heads // (QH // KVH)) * HD
    kv_block = jnp.minimum(kv_col // 128, w_key.shape[1] // 128 - 2)
    place = jnp.stack([t_index, seq_index, kv_block, kv_col - kv_block * 128]).astype(jnp.int32)
    inverse_rate = jnp.power(
        jnp.float32(rope_base), -(2.0 * jnp.arange(HD // 2, dtype=jnp.float32)) / HD
    )
    angles = inverse_rate[:, None] * places.astype(jnp.float32)[None, :]
    cos_t = jnp.cos(angles)
    sin_t = jnp.sin(angles)
    low_tiles = lower.reshape(n * chunks, QT)
    low_min = jnp.min(low_tiles, axis=1)
    low_max = jnp.max(low_tiles, axis=1)
    lower_row = lower.reshape(1, block_len)

    sets = [(first_half, list(range(m)), [0] * m)]
    for c in range(chunks):
        sets.append((gather_low(crossed[c], n), list(range(m, n)), [c * QT] * m))
    queries = []
    kv_sets = []
    spans = []
    for xs, pieces, offsets in sets:
        q_t, kv_t = project(
            place, xs, pieces, offsets, rows, gain_in, w_query, w_key, w_value, cos_t, sin_t, heads, groups
        )
        queries.append(q_t)
        held = [kv_t]
        for d in range(1, reach + 1):
            held.append(
                lax.ppermute(kv_t, "seq", [(i, i + d) for i in range(seq_count - d)])
            )
        kv_sets.append(held)
        lane = 0
        here = []
        for x, piece, offset in zip(xs, pieces, offsets):
            here.append((lane, piece * rows + offset, x.shape[0]))
            lane += x.shape[0]
        spans.append(here)
    kv_lists = [[held[d] for held in kv_sets] for d in range(reach + 1)]
    layout = [spans] * (reach + 1)

    sums = []
    for c in range(chunks):
        head_rows = attend(
            place,
            low_min,
            low_max,
            queries[0],
            queries[1 + c],
            lower_row,
            kv_lists,
            layout,
            groups,
            per,
            n,
            rows,
            order,
            c,
            chunks,
        )
        half = head_rows.shape[0] // 2
        sent = jnp.dot(head_rows[:half], w_out, preferred_element_type=jnp.float32).astype(jnp.bfloat16)
        kept = jnp.dot(head_rows[half:], w_out, preferred_element_type=jnp.float32).astype(jnp.bfloat16)
        mine = reduce_low(sent, kept, n).astype(jnp.bfloat16)
        theirs = flip(mine, "tensor", m)
        sums.append((mine, theirs))

    results = []
    for c in range(chunks):
        mine, theirs = sums[c]
        residual, mixed = merge(own, c, crossed[c], mine, theirs, gain_mlp)
        parts = [mixed]
        for bit in reversed(low_bits(n)):
            parts = [flip(part, "tensor", bit) for part in parts] + parts
        sent, kept = feed_forward(parts, w_gate, w_up, w_down)
        down = reduce_low(sent, kept, n)
        other = flip(down[QT:].astype(jnp.bfloat16), "tensor", m)
        results.append(
            (residual + (down[:QT] + other.astype(jnp.float32))).astype(jnp.bfloat16)
        )
    return jnp.concatenate(results, axis=0), sums[-1][0]


def hand_over(cache_pool, req_len, req_owner, block_list, after):
    owners = lax.axis_size("seq") * lax.axis_size("dec")
    me = lax.axis_index("seq") * lax.axis_size("dec") + lax.axis_index("dec")
    outgoing = pack_cache(
        me.reshape(1).astype(jnp.int32), cache_pool, req_len, req_owner, block_list, owners
    )
    outgoing, _ = lax.optimization_barrier((outgoing, after))
    decode = jnp.zeros((owners * PAIR,) + outgoing[0].shape[1:], jnp.bfloat16)
    for k in range(owners):
        got = outgoing[k] if k == 0 else flip(outgoing[k], ("seq", "dec"), k)
        start = jnp.bitwise_xor(me, k) * PAIR
        decode = lax.dynamic_update_slice_in_dim(decode, got, start, 0)
    return decode


def from_behind(value, axis, steps):
    count = lax.axis_size(axis)
    leading, last = (max(0, -steps), min(count, count - steps))
    return lax.ppermute(value, axis, [(source, source + steps) for source in range(leading, last)])


def plain_rms_scale(row_block, gain_vec):
    values = row_block.astype(jnp.float32)
    mean_square = jnp.mean(values * values, axis=-1, keepdims=True)
    return values * lax.rsqrt(mean_square + norm_eps) * gain_vec


def rotate(values, places):
    half_dim = values.shape[-1] // 2
    inverse_rate = jnp.power(
        jnp.float32(rope_base), -(2.0 * jnp.arange(half_dim, dtype=jnp.float32)) / values.shape[-1]
    )
    angles = places.astype(jnp.float32)[:, None] * inverse_rate[None, :]
    cosine = jnp.cos(angles)[:, None, :]
    sine_vals = jnp.sin(angles)[:, None, :]
    first_half = values[..., :half_dim]
    second = values[..., half_dim:]
    return jnp.concatenate(
        [first_half * cosine - second * sine_vals, second * cosine + first_half * sine_vals],
        axis=-1,
    )


def plain_hand_over(cache_pool, req_len, req_owner, block_list):
    pool_len = cache_pool.shape[0]
    layers_here = cache_pool.shape[1]
    pieces = cache_pool.shape[2]
    req_count = req_len.shape[1]
    owner_count = lax.axis_size("seq") * lax.axis_size("dec")
    max_blocks = MAXLEN // BT
    lengths = req_len[0]
    owner_ids = req_owner[:, 0]
    listing = block_list[0]
    req_order = jnp.arange(req_count, dtype=jnp.int32)
    counts = (lengths + BT - 1) // BT
    first_block = jnp.cumsum(counts) - counts
    same_owner = (owner_ids[:, None] == owner_ids[None, :]) & (
        req_order[None, :] < req_order[:, None]
    )
    arrival = jnp.sum(same_owner.astype(jnp.int32), axis=1)
    block_idx = jnp.minimum(
        first_block[:, None] + jnp.arange(max_blocks, dtype=jnp.int32)[None, :], pool_len - 1
    )
    picked = cache_pool[listing[block_idx]].reshape(
        req_count, max_blocks, layers_here, pieces, BT, HD
    )
    token_idx = (
        jnp.arange(max_blocks, dtype=jnp.int32)[:, None] * BT
        + jnp.arange(BT, dtype=jnp.int32)[None, :]
    )
    keep_mask = token_idx[None] < lengths[:, None, None]
    picked = jnp.where(keep_mask[:, :, None, None, :, None], picked, jnp.zeros((), jnp.bfloat16))
    arranged = jnp.transpose(picked, (0, 2, 3, 1, 4, 5)).reshape(
        req_count, layers_here, pieces, MAXLEN * HD
    )
    slot_owner = jnp.arange(owner_count, dtype=jnp.int32)[:, None, None]
    slot_rank = jnp.arange(PAIR, dtype=jnp.int32)[None, :, None]
    matches = (owner_ids[None, None, :] == slot_owner) & (arrival[None, None, :] == slot_rank)
    source_req = jnp.sum(jnp.where(matches, req_order[None, None, :], 0), axis=-1)
    filled = jnp.any(matches, axis=-1)
    outgoing = jnp.where(
        filled[:, :, None, None, None], arranged[source_req], jnp.zeros((), jnp.bfloat16)
    )
    arrived = lax.all_to_all(outgoing, ("seq", "dec"), split_axis=0, concat_axis=0, tiled=True)
    return arrived.reshape(owner_count * PAIR, layers_here, pieces, MAXLEN * HD)


def plain_shards(
    tokens,
    attn_gain,
    w_query,
    w_key,
    w_value,
    w_out,
    mlp_gain,
    w_gate,
    w_up,
    w_down,
    positions,
    window_lo,
    cache_pool,
    req_len,
    req_owner,
    block_list,
):
    decode_cache = plain_hand_over(cache_pool, req_len, req_owner, block_list)
    own_rows = tokens[0, 0]
    places = positions[0, 0]
    lower = window_lo[0, 0]
    block_len = places.shape[0]
    row_count = own_rows.shape[0]
    tensor_index = lax.axis_index("tensor")
    seq_index = lax.axis_index("seq")
    head_count = w_query.shape[1] // HD
    group_size = QH // KVH
    kv_count = max(1, head_count // group_size)
    kv_first = tensor_index * head_count // group_size
    key_cols = lax.dynamic_slice_in_dim(w_key, kv_first * HD, kv_count * HD, 1)
    value_cols = lax.dynamic_slice_in_dim(w_value, kv_first * HD, kv_count * HD, 1)
    w_joint = jnp.concatenate([w_query, key_cols, value_cols], axis=1)
    normed_in = plain_rms_scale(own_rows, attn_gain).astype(jnp.bfloat16)
    projected = jnp.dot(
        lax.all_gather(normed_in, "tensor", axis=0, tiled=True),
        w_joint,
        preferred_element_type=jnp.float32,
    )
    q_width = head_count * HD
    k_width = kv_count * HD
    queries = rotate(projected[:, :q_width].reshape(block_len, head_count, HD), places).astype(
        jnp.bfloat16
    )
    key_rot = rotate(
        projected[:, q_width : q_width + k_width].reshape(block_len, kv_count, HD), places
    ).astype(jnp.bfloat16)
    value_rows = (
        projected[:, q_width + k_width :].reshape(block_len, kv_count, HD).astype(jnp.bfloat16)
    )
    reach = WINDOW // block_len
    key_list = []
    value_list = []
    for distance in range(reach, 0, -1):
        earlier_keys, earlier_values = from_behind((key_rot, value_rows), "seq", distance)
        key_list.append(earlier_keys)
        value_list.append(earlier_values)
    all_keys = jnp.concatenate(key_list + [key_rot], axis=0)
    all_values = jnp.concatenate(value_list + [value_rows], axis=0)
    qblock = min(512, block_len)
    per_kv = head_count // kv_count
    score_scale = HD ** (-0.5)
    head_blocks = []
    for block_num in range(block_len // qblock):
        block_begin = block_num * qblock
        q_part = queries[block_begin : block_begin + qblock].reshape(qblock, kv_count, per_kv, HD)
        k_part = all_keys[block_begin : block_begin + WINDOW + qblock]
        v_part = all_values[block_begin : block_begin + WINDOW + qblock]
        scores = (
            jnp.einsum("qcgd,kcd->cgqk", q_part, k_part, preferred_element_type=jnp.float32)
            * score_scale
        )
        key_pos = (
            seq_index * block_len
            - WINDOW
            + block_begin
            + jnp.arange(WINDOW + qblock, dtype=jnp.int32)
        )
        query_pos = seq_index * block_len + block_begin + jnp.arange(qblock, dtype=jnp.int32)
        low_bound = lower[block_begin : block_begin + qblock]
        visible = (key_pos[None, :] >= low_bound[:, None]) & (
            key_pos[None, :] <= query_pos[:, None]
        )
        scores = jnp.where(visible[None, None], scores, -jnp.inf)
        row_top = jnp.max(scores, axis=-1, keepdims=True)
        exp_scores = jnp.exp(scores - row_top)
        row_total = jnp.sum(exp_scores, axis=-1, keepdims=True)
        weights = (exp_scores / row_total).astype(jnp.bfloat16)
        mixed_vals = jnp.einsum(
            "cgqk,kcd->qcgd", weights, v_part, preferred_element_type=jnp.float32
        )
        head_blocks.append(mixed_vals.reshape(qblock, q_width).astype(jnp.bfloat16))
    heads = jnp.concatenate(head_blocks, axis=0)
    w_pair = jnp.concatenate([w_gate, w_up], axis=1)
    unit_count = w_gate.shape[1]
    attn_share = lax.psum_scatter(
        jnp.dot(heads, w_out, preferred_element_type=jnp.float32).astype(jnp.bfloat16),
        "tensor",
        scatter_dimension=0,
        tiled=True,
    ).astype(jnp.float32)
    residual = own_rows.astype(jnp.float32) + attn_share
    gate_up = jnp.dot(
        lax.all_gather(
            plain_rms_scale(residual, mlp_gain).astype(jnp.bfloat16), "tensor", axis=0, tiled=True
        ),
        w_pair,
        preferred_element_type=jnp.float32,
    )
    hidden = (jax.nn.silu(gate_up[:, :unit_count]) * gate_up[:, unit_count:]).astype(jnp.bfloat16)
    mixed = lax.psum_scatter(
        jnp.dot(hidden, w_down, preferred_element_type=jnp.float32).astype(jnp.bfloat16),
        "tensor",
        scatter_dimension=0,
        tiled=True,
    ).astype(jnp.float32)
    layer_out = (residual + mixed).astype(jnp.bfloat16).reshape(1, 1, row_count, own_rows.shape[1])
    return (layer_out, decode_cache)


def shards(
    tokens,
    attn_gain,
    w_query,
    w_key,
    w_value,
    w_out,
    mlp_gain,
    w_gate,
    w_up,
    w_down,
    positions,
    window_lo,
    cache_pool,
    req_len,
    req_owner,
    block_list,
):
    own = tokens[0, 0]
    if own.shape[0] % QT or lax.axis_size("tensor") < 4:
        return plain_shards(
            tokens,
            attn_gain,
            w_query,
            w_key,
            w_value,
            w_out,
            mlp_gain,
            w_gate,
            w_up,
            w_down,
            positions,
            window_lo,
            cache_pool,
            req_len,
            req_owner,
            block_list,
        )
    layer_out, after = layer(
        own,
        attn_gain,
        w_query,
        w_key,
        w_value,
        w_out,
        mlp_gain,
        w_gate,
        w_up,
        w_down,
        positions[0, 0],
        window_lo[0, 0],
    )
    decode = hand_over(cache_pool, req_len, req_owner, block_list, after)
    return (layer_out.reshape(1, 1, *own.shape), decode)


def solution(mesh):
    in_specs = (
        P("dec", "seq", "tensor", None),
        P(),
        P(None, "tensor"),
        P(),
        P(),
        P("tensor", None),
        P(),
        P(None, "tensor"),
        P(None, "tensor"),
        P("tensor", None),
        P("dec", "seq", None),
        P("dec", "seq", None),
        P(("seq", "dec"), None, "tensor", None),
        P(("seq", "dec"), None),
        P(("seq", "dec"), None),
        P(("seq", "dec"), None),
    )
    out_specs = (P("dec", "seq", "tensor", None), P(("seq", "dec"), None, "tensor", None))
    return jax.shard_map(shards, mesh=mesh, in_specs=in_specs, out_specs=out_specs, check_vma=False)
```
